32 devices in a mesh: parts: 2 (over x), mesh: 16 (over z, y, core).
Axes of the slice: x: 2, y: 2, z: 4, core: 2. Of those that a mesh axis runs over, the one named last changes fastest.
Arguments:
- grid_in: bfloat16 [474, 8192], P(None, ('parts', 'mesh')), parts along dimension 1, may hold values from -6 to 6
- mesh_init: bfloat16 [512, 512], P(('parts', 'mesh')), parts along dimension 0, may hold values from -6 to 6
- embed_weight: bfloat16 [474, 512], replicated, may hold values from -0.25 to 0.25
- enc_send: bfloat16 [512, 512], replicated, may hold values from -0.25 to 0.25
- enc_recv: bfloat16 [512, 512], replicated, may hold values from -0.25 to 0.25
- enc_node: bfloat16 [512, 512], replicated, may hold values from -0.25 to 0.25
- mid_send: bfloat16 [512, 512], replicated, may hold values from -0.25 to 0.25
- mid_recv: bfloat16 [512, 512], replicated, may hold values from -0.25 to 0.25
- mid_node: bfloat16 [512, 512], replicated, may hold values from -0.25 to 0.25
- dec_send: bfloat16 [512, 512], replicated, may hold values from -0.25 to 0.25
- dec_recv: bfloat16 [512, 512], replicated, may hold values from -0.25 to 0.25
- dec_node: bfloat16 [512, 512], replicated, may hold values from -0.25 to 0.25
- mid_gain: float32 [512], replicated, may hold values from 0.5 to 1.5
- cotangent: bfloat16 [8192, 512], P(('parts', 'mesh')), parts along dimension 0, may hold values from -0.035888672 to 0.035888672
- enc_from: int32 [48, 256], P('mesh'), may hold values from 0 to 255
- enc_into: int32 [48, 256], P('mesh'), may hold values from 0 to 15
- enc_count: int32 [48], P('mesh'), may hold values from 1 to 256, as said below
- mid_from: int32 [256, 32], P('mesh'), may hold values from 0 to 15
- mid_into: int32 [256, 32], P('mesh'), may hold values from 0 to 15
- mid_count: int32 [256], P('mesh'), may hold values from 0 to 32, as said below
- dec_from: int32 [48, 512], P('mesh'), may hold values from 0 to 15
- dec_into: int32 [48, 512], P('mesh'), may hold values from 0 to 255
- dec_count: int32 [48], P('mesh'), may hold values from 1 to 512, as said below
Outputs:
- update: bfloat16 [8192, 512], P(('parts', 'mesh')), parts along dimension 0
- embed_grad: float32 [948, 512], P('parts'), parts along dimension 0
- encode_grad: float32 [1024, 512], P('parts'), parts along dimension 0
- process_grad: float32 [1024, 512], P('parts'), parts along dimension 0
- decode_grad: float32 [1024, 512], P('parts'), parts along dimension 0
- output_grad: float32 [1024, 512], P('parts'), parts along dimension 0
The draws below stay inside these ranges and needn't reach their ends.
There are 2 independent parts, one for each index of `parts`. The reference program is written for one: setup_inputs(seed, part) draws one part's arguments, and reference() takes and returns one part's arrays. A program takes and returns all parts, laid end to end along the dimension named above; an argument that names none is the same for every part. Nothing has to cross between parts.
Inputs may be any that keep to these rules, and one draw needn't show every extreme that they name: `enc_count`: at most 256; in every draw one destination block is full from each of its 3 neighbouring source blocks. `mid_count`: at most 32; in every draw one destination block is full from every source block. `dec_count`: at most 512; in every draw one destination block is full from each of its 3 neighbouring source blocks.
All inputs are finite; a program needn't handle non-finite values.
Results may differ from the reference program's by a relative error of at most 0.018.
Values may be sent and summed in bfloat16 or wider, within the bound.
A program may use at most 64 MiB of HBM per device.

```python
import jax
import jax.numpy as jnp
from jax import lax

D = 512
CH = 474
SPAN = 3
GRID_DEV = 256
MESH_DEV = 16
CAP_ENC = 256
CAP_DEC = 512
BLOCKS = 16
PAIRS = 256
NEAR = 48
CAP_MID = 32
GRID = 4096
MESH = 256


def skewed_counts(key, cap, columns, lowest):
    keys = jax.random.split(key, 4)
    light = jax.random.randint(keys[0], (BLOCKS, columns), lowest, cap // 2 + 1)
    heavy = cap - jax.random.randint(keys[1], (BLOCKS, columns), 0, cap // 4 + 1)
    busy = jax.random.randint(keys[2], (BLOCKS, 1), 0, 4) == 0
    counts = jnp.where(busy, heavy, light)
    chosen = jax.random.randint(keys[3], (), 0, BLOCKS)
    places = lax.broadcasted_iota(jnp.int32, (BLOCKS, columns), 0)
    counts = jnp.where(places == chosen, cap, counts)
    return counts.reshape(-1).astype(jnp.int32)


def draw_enc_count(key, part):
    return skewed_counts(jax.random.fold_in(key, 101), CAP_ENC, SPAN, 1)


def draw_mid_count(key, part):
    return skewed_counts(jax.random.fold_in(key, 202), CAP_MID, BLOCKS, 0)


def draw_dec_count(key, part):
    return skewed_counts(jax.random.fold_in(key, 303), CAP_DEC, SPAN, 1)


def touch_ends(values, own_key, low, high):
    longest = values.shape.index(max(values.shape))
    spots = []
    for shift in (0, 1):
        where = [jax.random.randint(jax.random.fold_in(own_key, axis), (), 0, length) for axis, length in enumerate(values.shape)]
        where[longest] = (where[longest] + shift) % values.shape[longest]
        spots.append(tuple(where))
    return values.at[spots[0]].set(low).at[spots[1]].set(high)


def block_levels(key, dims, cuts, least, top_value):
    def one(dim, shards_of):
        steps = jax.random.uniform(jax.random.fold_in(jax.random.fold_in(key, 6), dim), (shards_of,), jnp.float32, least / len(cuts), top_value / len(cuts))
        return jnp.repeat(jnp.exp(steps), dims[dim] // shards_of).reshape((-1,) + (1,) * (len(dims) - dim - 1))

    gain = one(*cuts[0])
    for cut in cuts[1:]:
        gain = gain * one(*cut)
    return gain


def scatter_about(stream_key, dims, scale, bound, shards=(), held_as=jnp.bfloat16):
    drawn = jax.random.normal(stream_key, dims, jnp.float32) * scale
    if len(shards) > 0:
        drawn = block_levels(stream_key, dims, shards, -0.22, 0.18) * drawn
    return jnp.clip(drawn, min=-bound, max=bound).astype(held_as)


def setup_inputs(seed: int = 0, part: int = 0) -> dict:
    seeds = jax.random.split(jax.random.key(seed), 24)
    part_keys = jax.random.split(jax.random.fold_in(seeds[23], part), 24)
    grid_in = scatter_about(part_keys[0], (CH, GRID), 1.0, 6.0, ((1, 16),))
    mesh_init = scatter_about(part_keys[1], (MESH, D), 1.0, 6.0, ((0, 16),))
    embed_weight = scatter_about(seeds[2], (CH, D), CH ** -0.5, 0.25)
    enc_send = scatter_about(seeds[3], (D, D), D ** -0.5, 0.25)
    enc_recv = scatter_about(seeds[4], (D, D), D ** -0.5, 0.25)
    enc_node = scatter_about(seeds[5], (D, D), D ** -0.5, 0.25)
    mid_send = scatter_about(seeds[6], (D, D), D ** -0.5, 0.25)
    mid_recv = scatter_about(seeds[7], (D, D), D ** -0.5, 0.25)
    mid_node = scatter_about(seeds[8], (D, D), D ** -0.5, 0.25)
    dec_send = scatter_about(seeds[9], (D, D), D ** -0.5, 0.25)
    dec_recv = scatter_about(seeds[10], (D, D), D ** -0.5, 0.25)
    dec_node = scatter_about(seeds[11], (D, D), D ** -0.5, 0.25)
    mid_gain = jnp.clip(jax.random.uniform(seeds[12], (D,), jnp.float32, 0.5, 1.5), 0.5, 1.5)
    cotangent = scatter_about(part_keys[13], (GRID, D), 0.006, 0.035888672, ((0, 16),))
    enc_from = touch_ends(jax.random.randint(seeds[14], (NEAR, CAP_ENC), 0, GRID_DEV), jax.random.fold_in(seeds[14], 1), 0, GRID_DEV - 1).astype(jnp.int32)
    enc_into = touch_ends(jax.random.randint(seeds[15], (NEAR, CAP_ENC), 0, MESH_DEV), jax.random.fold_in(seeds[15], 1), 0, MESH_DEV - 1).astype(jnp.int32)
    enc_count = draw_enc_count(jax.random.fold_in(seeds[23], 71), part)
    mid_from = touch_ends(jax.random.randint(seeds[17], (PAIRS, CAP_MID), 0, MESH_DEV), jax.random.fold_in(seeds[17], 1), 0, MESH_DEV - 1).astype(jnp.int32)
    mid_into = touch_ends(jax.random.randint(seeds[18], (PAIRS, CAP_MID), 0, MESH_DEV), jax.random.fold_in(seeds[18], 1), 0, MESH_DEV - 1).astype(jnp.int32)
    mid_count = draw_mid_count(jax.random.fold_in(seeds[23], 71), part)
    dec_from = touch_ends(jax.random.randint(seeds[20], (NEAR, CAP_DEC), 0, MESH_DEV), jax.random.fold_in(seeds[20], 1), 0, MESH_DEV - 1).astype(jnp.int32)
    dec_into = touch_ends(jax.random.randint(seeds[21], (NEAR, CAP_DEC), 0, GRID_DEV), jax.random.fold_in(seeds[21], 1), 0, GRID_DEV - 1).astype(jnp.int32)
    dec_count = draw_dec_count(jax.random.fold_in(seeds[23], 71), part)
    return dict(grid_in=grid_in, mesh_init=mesh_init, embed_weight=embed_weight, enc_send=enc_send, enc_recv=enc_recv, enc_node=enc_node, mid_send=mid_send, mid_recv=mid_recv, mid_node=mid_node, dec_send=dec_send, dec_recv=dec_recv, dec_node=dec_node, mid_gain=mid_gain, cotangent=cotangent, enc_from=enc_from, enc_into=enc_into, enc_count=enc_count, mid_from=mid_from, mid_into=mid_into, mid_count=mid_count, dec_from=dec_from, dec_into=dec_into, dec_count=dec_count)


EPSILON = 1e-05

def layer_norm(values):
    center = values - lax.optimization_barrier(jnp.mean(values, axis=-1, keepdims=True))
    spread = lax.optimization_barrier(jnp.mean(center * center, axis=-1, keepdims=True))
    return center * lax.rsqrt(spread + EPSILON)

def silu_slope(values):
    sigma = jax.nn.sigmoid(values)
    return sigma * (1.0 + values * (1.0 - sigma))

def live_slots(count, cap):
    return jnp.arange(cap, dtype=jnp.int32)[None, None, :] < count.reshape(BLOCKS, -1)[:, :, None]

def aggregate(sender, target, source_idx, local_idx, alive, rows):
    width = sender.shape[1]

    def block(pieces):
        from_rows, into_rows, valid, which = pieces
        targets = lax.dynamic_slice_in_dim(target, which * rows, rows, 0)
        inputs = sender[from_rows].astype(jnp.float32) + targets[into_rows].astype(jnp.float32)
        message = jax.nn.silu(inputs).astype(jnp.bfloat16)
        message = lax.optimization_barrier(message).astype(jnp.float32)
        message = jnp.where(valid[..., None], message, 0.0)
        return jax.ops.segment_sum(message.reshape(-1, width), into_rows.reshape(-1), num_segments=rows)
    blocks = jnp.arange(BLOCKS, dtype=jnp.int32)
    return lax.map(block, (source_idx, local_idx, alive, blocks)).reshape(-1, width)

def edge_back(sender, target, source_idx, local_idx, alive, rows, grad_agg):
    width = sender.shape[1]

    def block(carry, pieces):
        from_rows, into_rows, valid, which = pieces
        targets = lax.dynamic_slice_in_dim(target, which * rows, rows, 0)
        grads = lax.dynamic_slice_in_dim(grad_agg, which * rows, rows, 0)
        inputs = sender[from_rows].astype(jnp.float32) + targets[into_rows].astype(jnp.float32)
        grad_in = jnp.where(valid[..., None], grads[into_rows].astype(jnp.float32) * silu_slope(inputs), 0.0)
        grad_in = lax.optimization_barrier(grad_in.astype(jnp.bfloat16)).astype(jnp.float32)
        flat = grad_in.reshape(-1, width)
        carry = carry.at[from_rows.reshape(-1)].add(flat)
        grad_dst = jax.ops.segment_sum(flat, into_rows.reshape(-1), num_segments=rows)
        return (carry, grad_dst)
    blocks = jnp.arange(BLOCKS, dtype=jnp.int32)
    start = jnp.zeros((sender.shape[0], width), jnp.float32)
    total, parts = lax.scan(block, start, (source_idx, local_idx, alive, blocks))
    return (total, parts.reshape(-1, width))

def mm(left, right):
    return jnp.dot(left, right, preferred_element_type=jnp.float32)

def reference(grid_in, mesh_init, embed_weight, enc_send, enc_recv, enc_node, mid_send, mid_recv, mid_node, dec_send, dec_recv, dec_node, mid_gain, cotangent, enc_from, enc_into, enc_count, mid_from, mid_into, mid_count, dec_from, dec_into, dec_count):
    blocks = jnp.arange(BLOCKS, dtype=jnp.int32)
    neighbours = ((blocks[:, None] + jnp.arange(SPAN, dtype=jnp.int32)[None, :] + (BLOCKS - 1)) % BLOCKS).astype(jnp.int32)
    enc_src = (enc_from.reshape(BLOCKS, SPAN, CAP_ENC) + neighbours[:, :, None] * GRID_DEV).astype(jnp.int32)
    enc_dst = enc_into.reshape(BLOCKS, SPAN, CAP_ENC)
    enc_live = live_slots(enc_count, CAP_ENC)
    mid_src = (mid_from.reshape(BLOCKS, BLOCKS, CAP_MID) + blocks[None, :, None] * MESH_DEV).astype(jnp.int32)
    mid_dst = mid_into.reshape(BLOCKS, BLOCKS, CAP_MID)
    mid_live = live_slots(mid_count, CAP_MID)
    dec_src = (dec_from.reshape(BLOCKS, SPAN, CAP_DEC) + neighbours[:, :, None] * MESH_DEV).astype(jnp.int32)
    dec_dst = dec_into.reshape(BLOCKS, SPAN, CAP_DEC)
    dec_live = live_slots(dec_count, CAP_DEC)
    pre_act = mm(grid_in.T, embed_weight)
    hidden = jax.nn.silu(pre_act).astype(jnp.bfloat16)
    enc_proj = mm(hidden, enc_send).astype(jnp.bfloat16)
    enc_target = mm(mesh_init, enc_recv).astype(jnp.bfloat16)
    enc_agg = aggregate(enc_proj, enc_target, enc_src, enc_dst, enc_live, MESH_DEV)
    enc_norm = layer_norm(enc_agg).astype(jnp.bfloat16)
    latent = (mesh_init.astype(jnp.float32) + mm(enc_norm, enc_node)).astype(jnp.bfloat16)
    mid_proj = mm(latent, mid_send).astype(jnp.bfloat16)
    mid_target = mm(latent, mid_recv).astype(jnp.bfloat16)
    mid_agg = aggregate(mid_proj, mid_target, mid_src, mid_dst, mid_live, MESH_DEV)
    mid_norm = (layer_norm(mid_agg) * mid_gain).astype(jnp.bfloat16)
    latent_two = (latent.astype(jnp.float32) + mm(mid_norm, mid_node)).astype(jnp.bfloat16)
    dec_proj = mm(latent_two, dec_send).astype(jnp.bfloat16)
    dec_target = mm(hidden, dec_recv).astype(jnp.bfloat16)
    dec_agg = aggregate(dec_proj, dec_target, dec_src, dec_dst, dec_live, GRID_DEV)
    dec_norm = layer_norm(dec_agg).astype(jnp.bfloat16)
    update = (hidden.astype(jnp.float32) + mm(dec_norm, dec_node)).astype(jnp.bfloat16)
    output_grad = mm(dec_norm.T, cotangent)
    pull = jax.vjp(layer_norm, dec_agg)[1]
    dec_cot = pull(mm(cotangent, dec_node.T))[0].astype(jnp.bfloat16)
    dec_src_sum, dec_dst_sum = edge_back(dec_proj, dec_target, dec_src, dec_dst, dec_live, GRID_DEV, dec_cot)
    dec_src_grad = dec_src_sum.astype(jnp.bfloat16)
    dec_dst_grad = dec_dst_sum.astype(jnp.bfloat16)
    decode_grad = mm(latent_two.T, dec_src_grad)
    latent_two_grad = mm(dec_src_grad, dec_send.T)
    pull = jax.vjp(lambda values: layer_norm(values) * mid_gain, mid_agg)[1]
    mid_cot = pull(mm(latent_two_grad.astype(jnp.bfloat16), mid_node.T))[0].astype(jnp.bfloat16)
    mid_src_sum, mid_dst_sum = edge_back(mid_proj, mid_target, mid_src, mid_dst, mid_live, MESH_DEV, mid_cot)
    mid_src_grad = mid_src_sum.astype(jnp.bfloat16)
    mid_dst_grad = mid_dst_sum.astype(jnp.bfloat16)
    process_grad = mm(latent.T, mid_src_grad)
    latent_grad = (latent_two_grad + mm(mid_src_grad, mid_send.T) + mm(mid_dst_grad, mid_recv.T)).astype(jnp.bfloat16)
    pull = jax.vjp(layer_norm, enc_agg)[1]
    enc_cot = pull(mm(latent_grad, enc_node.T))[0].astype(jnp.bfloat16)
    enc_src_sum, unused_dst = edge_back(enc_proj, enc_target, enc_src, enc_dst, enc_live, MESH_DEV, enc_cot)
    enc_src_grad = enc_src_sum.astype(jnp.bfloat16)
    encode_grad = mm(hidden.T, enc_src_grad)
    hidden_grad = cotangent.astype(jnp.float32) + mm(enc_src_grad, enc_send.T) + mm(dec_dst_grad, dec_recv.T)
    pre_grad = (hidden_grad * silu_slope(pre_act)).astype(jnp.bfloat16)
    embed_grad = mm(grid_in, pre_grad)
    return (update, embed_grad, encode_grad, process_grad, decode_grad, output_grad)
```

```python
import jax
import jax.numpy as jnp
from jax import lax
from jax.sharding import PartitionSpec as P

EPSILON = 1e-05


def with_halo(cells, sides, width):
    for axis, dim in sides:
        count = lax.axis_size(axis)
        head = lax.slice_in_dim(cells, 0, width, axis=dim)
        tail = lax.slice_in_dim(cells, cells.shape[dim] - width, cells.shape[dim], axis=dim)
        cells = jnp.concatenate(
            [
                lax.ppermute(tail, axis, [(i, (i + 1) % count) for i in range(count)]),
                cells,
                lax.ppermute(head, axis, [((i + 1) % count, i) for i in range(count)]),
            ],
            axis=dim,
        )
    return cells


def shifted(shard, axis, by):
    count = lax.axis_size(axis)
    return lax.ppermute(shard, axis, [(i, (i + by) % count) for i in range(count)])


def layer_norm(values):
    center = values - jnp.mean(values, axis=-1, keepdims=True)
    spread = jnp.mean(center * center, axis=-1, keepdims=True)
    return center * lax.rsqrt(spread + EPSILON)


def silu_slope(values):
    sigma = jax.nn.sigmoid(values)
    return sigma * (1.0 + values * (1.0 - sigma))


def mm(left, right):
    return jnp.dot(left, right, preferred_element_type=jnp.float32)


def mm_right_t(left, right):
    return jnp.einsum("ae,de->ad", left, right, preferred_element_type=jnp.float32)


def mm_left_t(left, right):
    return jnp.einsum("ad,ae->de", left, right, preferred_element_type=jnp.float32)


def selector(index, valid, rows):
    flat = index.reshape(-1)
    picks = lax.broadcasted_iota(jnp.int32, (rows, flat.shape[0]), 0) == flat[None, :]
    if valid is not None:
        picks = picks & valid.reshape(-1)[None, :]
    return picks.astype(jnp.bfloat16)


def live_slots(index, count):
    return lax.broadcasted_iota(jnp.int32, index.shape, 1) < count[:, None]


def block_rows(index, rows):
    return lax.broadcasted_iota(jnp.int32, index.shape, 0) * rows + index


def collect(table, rows, shape):
    picked = jnp.einsum("rs,rd->sd", table, rows, preferred_element_type=jnp.float32)
    return picked.astype(jnp.bfloat16).reshape(shape + (rows.shape[1],))


def send_slots(block):
    return lax.all_to_all(block, "mesh", split_axis=0, concat_axis=0, tiled=True)


def margin(block):
    return with_halo(block, (("mesh", 0),), block.shape[0])


def return_margin(near_grad, rows):
    total = near_grad[rows : 2 * rows]
    for offset, piece in ((-1, near_grad[:rows]), (1, near_grad[2 * rows :])):
        total = total + shifted(piece.astype(jnp.bfloat16), "mesh", offset).astype(piece.dtype)
    return total


def edge_forward(arrived, target, table):
    width = arrived.shape[-1]
    target_at = jnp.einsum("rs,rd->sd", table, target, preferred_element_type=jnp.float32)
    inputs = arrived.reshape(-1, width).astype(jnp.float32) + target_at
    message = jax.nn.silu(inputs).astype(jnp.bfloat16)
    return (mm(table, message), inputs)


def edge_backward(grad_agg, inputs, table, shape):
    grad_at = jnp.einsum("rs,rd->sd", table, grad_agg, preferred_element_type=jnp.float32)
    grad_in = (grad_at * silu_slope(inputs)).astype(jnp.bfloat16)
    return (grad_in.reshape(shape), mm(table, grad_in))


def fetch(projected, asked):
    table = selector(asked, None, projected.shape[0])
    return (send_slots(collect(table, projected, asked.shape)), table)


def give_back(grad_slots, handle):
    width = grad_slots.shape[-1]
    returned = send_slots(grad_slots)
    return mm(handle, returned.reshape(-1, width))


def whole_rows(block):
    return lax.all_gather(block, "mesh", axis=0, tiled=True)


def summed(term):
    return lax.psum(term.astype(jnp.bfloat16), "mesh").astype(jnp.float32)


def shards(
    grid_in,
    mesh_init,
    embed_weight,
    enc_send,
    enc_recv,
    enc_node,
    mid_send,
    mid_recv,
    mid_node,
    dec_send,
    dec_recv,
    dec_node,
    mid_gain,
    cotangent,
    enc_from,
    enc_into,
    enc_count,
    mid_from,
    mid_into,
    mid_count,
    dec_from,
    dec_into,
    dec_count,
):
    grid_rows = grid_in.shape[1]
    mesh_rows = mesh_init.shape[0]
    mid_asked = lax.all_to_all(mid_from, "mesh", split_axis=0, concat_axis=0, tiled=True)
    pre_act = jnp.einsum("cg,cd->gd", grid_in, embed_weight, preferred_element_type=jnp.float32)
    hidden = jax.nn.silu(pre_act).astype(jnp.bfloat16)
    enc_proj = mm(hidden, enc_send).astype(jnp.bfloat16)
    enc_near = margin(enc_proj)
    enc_source = selector(block_rows(enc_from, grid_rows), None, enc_near.shape[0])
    enc_arrived = collect(enc_source, enc_near, enc_from.shape)
    enc_table = selector(enc_into, live_slots(enc_into, enc_count), mesh_rows)
    enc_target = mm(mesh_init, enc_recv).astype(jnp.bfloat16)
    enc_agg, enc_inputs = edge_forward(enc_arrived, enc_target, enc_table)
    enc_norm = layer_norm(enc_agg).astype(jnp.bfloat16)
    latent = (mesh_init.astype(jnp.float32) + mm(enc_norm, enc_node)).astype(jnp.bfloat16)
    mid_proj = mm(latent, mid_send).astype(jnp.bfloat16)
    mid_target = mm(latent, mid_recv).astype(jnp.bfloat16)
    mid_arrived, mid_handle = fetch(mid_proj, mid_asked)
    mid_table = selector(mid_into, live_slots(mid_into, mid_count), mesh_rows)
    mid_agg, mid_inputs = edge_forward(mid_arrived, mid_target, mid_table)
    mid_norm = (layer_norm(mid_agg) * mid_gain).astype(jnp.bfloat16)
    latent_two = (latent.astype(jnp.float32) + mm(mid_norm, mid_node)).astype(jnp.bfloat16)
    dec_proj = mm(latent_two, dec_send).astype(jnp.bfloat16)
    dec_target = mm(hidden, dec_recv).astype(jnp.bfloat16)
    dec_near = margin(dec_proj)
    dec_source = selector(block_rows(dec_from, mesh_rows), None, dec_near.shape[0])
    dec_arrived = collect(dec_source, dec_near, dec_from.shape)
    dec_table = selector(dec_into, live_slots(dec_into, dec_count), grid_rows)
    dec_agg, dec_inputs = edge_forward(dec_arrived, dec_target, dec_table)
    dec_norm = layer_norm(dec_agg).astype(jnp.bfloat16)
    update = (hidden.astype(jnp.float32) + mm(dec_norm, dec_node)).astype(jnp.bfloat16)
    output_term = mm_left_t(dec_norm, cotangent)
    pull = jax.vjp(layer_norm, dec_agg)[1]
    dec_cot = pull(mm_right_t(cotangent, dec_node))[0].astype(jnp.bfloat16)
    dec_slots, dec_dst_sum = edge_backward(dec_cot, dec_inputs, dec_table, dec_arrived.shape)
    dec_near_grad = mm(dec_source, dec_slots.reshape(-1, dec_slots.shape[-1]))
    dec_src_grad = return_margin(dec_near_grad, mesh_rows).astype(jnp.bfloat16)
    dec_dst_grad = dec_dst_sum.astype(jnp.bfloat16)
    latent_two_grad = mm_right_t(dec_src_grad, dec_send)
    pull = jax.vjp(lambda values: layer_norm(values) * mid_gain, mid_agg)[1]
    mid_cot = pull(mm_right_t(latent_two_grad.astype(jnp.bfloat16), mid_node))[0].astype(
        jnp.bfloat16
    )
    mid_slots, mid_dst_sum = edge_backward(mid_cot, mid_inputs, mid_table, mid_arrived.shape)
    mid_src_grad = give_back(mid_slots, mid_handle).astype(jnp.bfloat16)
    mid_dst_grad = mid_dst_sum.astype(jnp.bfloat16)
    latent_grad = (
        latent_two_grad + mm_right_t(mid_src_grad, mid_send) + mm_right_t(mid_dst_grad, mid_recv)
    ).astype(jnp.bfloat16)
    pull = jax.vjp(layer_norm, enc_agg)[1]
    enc_cot = pull(mm_right_t(latent_grad, enc_node))[0].astype(jnp.bfloat16)
    enc_slots, enc_dst_sum = edge_backward(enc_cot, enc_inputs, enc_table, enc_arrived.shape)
    enc_near_grad = mm(enc_source, enc_slots.reshape(-1, enc_slots.shape[-1]))
    enc_src_grad = return_margin(enc_near_grad, grid_rows).astype(jnp.bfloat16)
    encode_term = mm_left_t(hidden, enc_src_grad)
    hidden_grad = (
        cotangent.astype(jnp.float32)
        + mm_right_t(enc_src_grad, enc_send)
        + mm_right_t(dec_dst_grad, dec_recv)
    )
    pre_grad = (hidden_grad * silu_slope(pre_act)).astype(jnp.bfloat16)
    embed_term = jnp.einsum("cg,gd->cd", grid_in, pre_grad, preferred_element_type=jnp.float32)
    process_grad = mm_left_t(whole_rows(latent), whole_rows(mid_src_grad))
    decode_grad = mm_left_t(whole_rows(latent_two), whole_rows(dec_src_grad))
    output_grad = summed(output_term)
    encode_grad = summed(encode_term)
    embed_grad = summed(embed_term)
    return (update, embed_grad, encode_grad, process_grad, decode_grad, output_grad)


def solution(mesh):
    placed = (
        P(None, ("parts", "mesh")),
        P(("parts", "mesh"), None),
        P(),
        P(),
        P(),
        P(),
        P(),
        P(),
        P(),
        P(),
        P(),
        P(),
        P(),
        P(("parts", "mesh"), None),
        P("mesh", None),
        P("mesh", None),
        P("mesh"),
        P("mesh", None),
        P("mesh", None),
        P("mesh"),
        P("mesh", None),
        P("mesh", None),
        P("mesh"),
    )
    return jax.shard_map(
        shards,
        mesh=mesh,
        in_specs=placed,
        out_specs=(
            P(("parts", "mesh"), None),
            P("parts", None),
            P("parts", None),
            P("parts", None),
            P("parts", None),
            P("parts", None),
        ),
        check_vma=False,
    )
```

```python
import functools

import jax
import jax.numpy as jnp
from jax import lax
from jax.experimental import pallas as pl
from jax.experimental.pallas import tpu as pltpu
from jax.sharding import PartitionSpec as P

EPSILON = 1e-05
F32 = jnp.float32
BF16 = jnp.bfloat16


def dot(left, right, dims):
    return lax.dot_general(left, right, (dims, ((), ())), preferred_element_type=F32)


def mm(left, right):
    return dot(left, right, ((1,), (0,)))


def mm_right_t(left, right):
    return dot(left, right, ((1,), (1,)))


def mm_left_t(left, right):
    return dot(left, right, ((0,), (0,)))


def normed(values):
    center = values - jnp.mean(values, axis=-1, keepdims=True)
    scale = lax.rsqrt(jnp.mean(center * center, axis=-1, keepdims=True) + EPSILON)
    return center * scale, scale


def norm_pull(unit, scale, grad):
    inner = jnp.mean(grad * unit, axis=-1, keepdims=True)
    return scale * (grad - jnp.mean(grad, axis=-1, keepdims=True) - unit * inner)


def sigmoid(values):
    return 1.0 / (1.0 + jnp.exp(-values))


def silu(values):
    return values * sigmoid(values)


def silu_slope(values):
    sigma = sigmoid(values)
    return sigma * (1.0 + values * (1.0 - sigma))


def picks(index, rows):
    places = lax.broadcasted_iota(jnp.int32, (rows, index.shape[1]), 0)
    return jnp.where(places == index, 1.0, 0.0).astype(BF16)


def kernel(
    n,
    shard,
    grid_in,
    mesh_init,
    embed_weight,
    enc_send,
    enc_recv,
    enc_node,
    mid_send,
    mid_recv,
    mid_node,
    dec_send,
    dec_recv,
    dec_node,
    mid_gain,
    cotangent,
    enc_pack,
    mid_pack,
    dec_pack,
    update,
    embed_grad,
    encode_grad,
    process_grad,
    decode_grad,
    output_grad,
    pre_act,
    hidden,
    enc_proj,
    dec_target,
    packs,
    targets,
    enc_inputs,
    agg_parts,
    agg_near,
    lat_all,
    mid_inputs,
    lat2_all,
    dec_near,
    dec_inputs,
    dec_cot,
    dec_parts,
    dec_back,
    dec_dst,
    dsg_all,
    mid_parts,
    mid_back,
    msg_all,
    cots,
    enc_src,
    terms,
    halves,
    paired,
    arrived,
    whole,
    held_grad,
    held_dst,
    near_send,
    near_recv,
    all_send,
    all_recv,
    pair_sem,
    ring_send,
    ring_recv,
):
    me = lax.axis_index("mesh")
    left = lax.rem(me + n - 1, n)
    right = lax.rem(me + 1, n)
    core = lax.rem(me, 2)
    chip = me // 2
    chips = n // 2
    partner = me + 1 - 2 * core
    grid_rows = hidden.shape[0]
    mesh_rows, width = mesh_init.shape

    def remote(src, dst, send, recv, device):
        return pltpu.make_async_remote_copy(
            src_ref=src,
            dst_ref=dst,
            send_sem=send,
            recv_sem=recv,
            device_id={"mesh": device},
            device_id_type=pl.DeviceIdType.MESH,
        )

    def to_left(which, src, dst):
        return remote(src, dst, near_send.at[which, 0], near_recv.at[which, 1], left)

    def to_right(which, src, dst):
        return remote(src, dst, near_send.at[which, 1], near_recv.at[which, 0], right)

    def near_arrive(which, first, second):
        remote(first, first, near_send.at[which, 1], near_recv.at[which, 0], right).wait_recv()
        remote(second, second, near_send.at[which, 0], near_recv.at[which, 1], left).wait_recv()

    def gather_copy(which, table, owner, peer):
        return remote(
            table.at[owner], table.at[owner], all_send.at[which, peer], all_recv.at[which, owner], peer
        )

    def gather_start(which, table):
        @pl.loop(1, n)
        def _(step):
            gather_copy(which, table, me, lax.rem(me + step, n)).start()

    def gather_take(which, table, first, last):
        @pl.loop(first, last)
        def _(step):
            owner = lax.rem(me + step, n)
            gather_copy(which, table, owner, owner).wait_recv()

    def gather_sent(which, table):
        @pl.loop(1, n)
        def _(step):
            gather_copy(which, table, me, lax.rem(me + step, n)).wait_send()

    def pair_copy(k):
        return remote(terms.at[k, 1 - core], halves.at[k], pair_sem.at[k, 0], pair_sem.at[k, 1], partner)

    def ring_copy(k, src, dst, stage, peer, slot):
        return remote(src, dst, ring_send.at[k, stage, peer], ring_recv.at[k, stage, slot], 2 * peer + core)

    def put_term(k, value):
        rows = value.shape[0]
        value = value.astype(BF16)
        for o in range(n):
            low, high = o * shard, min((o + 1) * shard, rows)
            if high - low < shard:
                terms[k, o % 2, o // 2] = jnp.zeros((shard, width), BF16)
            if low < high:
                terms[k, o % 2, o // 2, 0 : high - low] = value[low:high]
        pair_copy(k).start()

    def scatter_start(k):
        pair_copy(k).wait()

        @pl.loop(0, chips)
        def _(i):
            both = terms[k, core, i].astype(F32) + halves[k, i].astype(F32)
            paired[k, i] = both.astype(BF16)

        @pl.loop(1, chips)
        def _(step):
            peer = lax.rem(chip + step, chips)
            ring_copy(k, paired.at[k, peer], arrived.at[k, chip], 0, peer, chip).start()

    def scatter_end(k):
        def add(step, total):
            peer = lax.rem(chip + step, chips)
            ring_copy(k, paired.at[k, peer], arrived.at[k, peer], 0, peer, peer).wait_recv()
            return total + arrived[k, peer].astype(F32)

        total = lax.fori_loop(1, chips, add, paired[k, chip].astype(F32))
        whole[k, core, chip] = total.astype(BF16)

        @pl.loop(1, chips)
        def _(step):
            peer = lax.rem(chip + step, chips)
            mine = whole.at[k, core, chip]
            ring_copy(k, mine, mine, 1, peer, chip).start()

    def final_copy(k, side):
        return remote(whole.at[k, side], whole.at[k, side], pair_sem.at[k, 2], pair_sem.at[k, 3], partner)

    def swap_start(k):
        @pl.loop(1, chips)
        def _(step):
            peer = lax.rem(chip + step, chips)
            theirs = whole.at[k, core, peer]
            ring_copy(k, theirs, theirs, 1, peer, peer).wait_recv()

        final_copy(k, core).start()

    def swap_end(k, out):
        final_copy(k, core).wait_send()
        final_copy(k, 1 - core).wait_recv()
        rows = out.shape[0]
        for o in range(n):
            low, high = o * shard, min((o + 1) * shard, rows)
            if low < high:
                out[low:high] = whole[k, o % 2, o // 2, 0 : high - low].astype(F32)

        @pl.loop(1, chips)
        def _(step):
            peer = lax.rem(chip + step, chips)
            ring_copy(k, paired.at[k, peer], arrived.at[k, chip], 0, peer, chip).wait_send()
            mine = whole.at[k, core, chip]
            ring_copy(k, mine, mine, 1, peer, chip).wait_send()

    barrier = pltpu.get_barrier_semaphore()

    @pl.loop(1, n)
    def _(step):
        pl.semaphore_signal(
            barrier,
            inc=1,
            device_id={"mesh": lax.rem(me + step, n)},
            device_id_type=pl.DeviceIdType.MESH,
        )

    targets[1] = mm(mesh_init[...], enc_recv[...]).astype(BF16)
    pl.semaphore_wait(barrier, n - 1)
    first = [
        to_left(0, enc_pack, packs.at[1]),
        to_right(0, enc_pack, packs.at[0]),
        to_left(1, targets.at[1], targets.at[2]),
        to_right(1, targets.at[1], targets.at[0]),
    ]
    for copy in first:
        copy.start()

    values = mm_left_t(grid_in[...], embed_weight[...])
    pre_act[...] = values
    hidden[...] = silu(values).astype(BF16)
    enc_proj[...] = mm(hidden[...], enc_send[...]).astype(BF16)
    dec_target[...] = mm(hidden[...], dec_recv[...]).astype(BF16)

    near_arrive(0, packs.at[0], packs.at[1])
    near_arrive(1, targets.at[0], targets.at[2])

    def enc_tables(k):
        pack, row = ((packs[0], 2), (enc_pack[...], 1), (packs[1], 0))[k]
        return (
            picks(pack[row : row + 1], grid_rows),
            picks(pack[row + 3 : row + 4], mesh_rows),
        )

    for k in range(3):
        source, table = enc_tables(k)
        inputs = mm_left_t(source, enc_proj[...]) + mm_left_t(table, targets[k])
        enc_inputs[k] = inputs
        agg_parts[k] = mm(table, silu(inputs).astype(BF16))
    agg_sends = [
        to_left(2, agg_parts.at[0], agg_near.at[1]),
        to_right(2, agg_parts.at[2], agg_near.at[0]),
    ]
    for copy in agg_sends:
        copy.start()
    near_arrive(2, agg_near.at[0], agg_near.at[1])
    enc_unit, enc_scale = normed(agg_parts[1] + agg_near[0] + agg_near[1])
    latent = (mesh_init[...].astype(F32) + mm(enc_unit.astype(BF16), enc_node[...])).astype(BF16)
    lat_all[me] = latent
    gather_start(0, lat_all)
    mid_target = mm(latent, mid_recv[...]).astype(BF16)
    mid_table = picks(mid_pack[1:2], mesh_rows)
    target_at = mm_left_t(mid_table, mid_target)
    gather_take(0, lat_all, 1, n)
    mid_proj = mm(lat_all[...].reshape(n * mesh_rows, width), mid_send[...]).astype(BF16)
    mid_source = picks(mid_pack[0:1], n * mesh_rows)
    inputs = mm_left_t(mid_source, mid_proj) + target_at
    mid_inputs[...] = inputs
    mid_unit, mid_scale = normed(mm(mid_table, silu(inputs).astype(BF16)))
    mid_norm = (mid_unit * mid_gain[...]).astype(BF16)
    latent_two = (latent.astype(F32) + mm(mid_norm, mid_node[...])).astype(BF16)
    lat2_all[me] = latent_two
    gather_start(1, lat2_all)
    dec_near[1] = mm(latent_two, dec_send[...]).astype(BF16)
    gather_take(1, lat2_all, 1, 2)
    gather_take(1, lat2_all, n - 1, n)
    dec_near[0] = mm(lat2_all[left], dec_send[...]).astype(BF16)
    dec_near[2] = mm(lat2_all[right], dec_send[...]).astype(BF16)

    def dec_forward(j, total):
        source = picks(dec_pack[j, 0:1], mesh_rows)
        table = picks(dec_pack[j, 1:2], grid_rows)
        inputs = mm_left_t(source, dec_near[j]) + mm_left_t(table, dec_target[...])
        dec_inputs[j] = inputs
        return total + mm(table, silu(inputs).astype(BF16))

    dec_agg = lax.fori_loop(0, 3, dec_forward, jnp.zeros((grid_rows, width), F32))
    unit, scale = normed(dec_agg)
    dec_norm = unit.astype(BF16)
    dec_cot[...] = norm_pull(unit, scale, mm_right_t(cotangent[...], dec_node[...])).astype(BF16)
    dec_dst[...] = jnp.zeros((grid_rows, width), F32)

    def dec_backward(j, carry):
        source = picks(dec_pack[j, 0:1], mesh_rows)
        table = picks(dec_pack[j, 1:2], grid_rows)
        grad = (mm_left_t(table, dec_cot[...]) * silu_slope(dec_inputs[j])).astype(BF16)
        dec_parts[j] = mm(source, grad)
        dec_dst[...] += mm(table, grad)
        return carry

    lax.fori_loop(0, 3, dec_backward, 0)
    dec_sends = [
        to_left(3, dec_parts.at[0], dec_back.at[1]),
        to_right(3, dec_parts.at[2], dec_back.at[0]),
    ]
    for copy in dec_sends:
        copy.start()
    put_term(0, mm_left_t(dec_norm, cotangent[...]))
    update[...] = (hidden[...].astype(F32) + mm(dec_norm, dec_node[...])).astype(BF16)
    near_arrive(3, dec_back.at[0], dec_back.at[1])
    dec_src = (dec_parts[1] + dec_back[0] + dec_back[1]).astype(BF16)
    latent_two_grad = mm_right_t(dec_src, dec_send[...])
    grad = mm_right_t(latent_two_grad.astype(BF16), mid_node[...]) * mid_gain[...]
    mid_cot = norm_pull(mid_unit, mid_scale, grad).astype(BF16)
    grad = (mm_left_t(mid_table, mid_cot) * silu_slope(mid_inputs[...])).astype(BF16)
    mid_parts[...] = mm(mid_source, grad).astype(BF16).reshape(n, mesh_rows, width)

    def back_copy(peer, slot):
        return remote(
            mid_parts.at[peer], mid_back.at[slot], all_send.at[2, peer], all_recv.at[2, slot], peer
        )

    @pl.loop(1, n)
    def _(step):
        back_copy(lax.rem(me + step, n), me).start()

    held_dst[...] = mm(mid_table, grad).astype(BF16)
    held_grad[...] = latent_two_grad
    dsg_all[me] = dec_src
    scatter_start(0)

    def back_add(step, total):
        peer = lax.rem(me + step, n)
        back_copy(peer, peer).wait_recv()
        return total + mid_back[peer].astype(F32)

    mid_src = lax.fori_loop(1, n, back_add, mid_parts[me].astype(F32)).astype(BF16)
    msg_all[me] = mid_src
    latent_grad = (
        held_grad[...]
        + mm_right_t(msg_all[me], mid_send[...])
        + mm_right_t(held_dst[...], mid_recv[...])
    ).astype(BF16)
    enc_cot = norm_pull(enc_unit, enc_scale, mm_right_t(latent_grad, enc_node[...])).astype(BF16)
    cots[1] = enc_cot
    cot_sends = [
        to_left(4, cots.at[1], cots.at[2]),
        to_right(4, cots.at[1], cots.at[0]),
    ]
    for copy in cot_sends:
        copy.start()
    gather_start(3, dsg_all)
    gather_start(4, msg_all)
    scatter_end(0)
    near_arrive(4, cots.at[0], cots.at[2])
    enc_src[...] = jnp.zeros((grid_rows, width), F32)
    for k in range(3):
        source, table = enc_tables(k)
        grad = (mm_left_t(table, cots[k]) * silu_slope(enc_inputs[k])).astype(BF16)
        enc_src[...] += mm(source, grad)
    enc_src_grad = enc_src[...].astype(BF16)
    put_term(1, mm_left_t(hidden[...], enc_src_grad))
    hidden_grad = (
        cotangent[...].astype(F32)
        + mm_right_t(enc_src_grad, enc_send[...])
        + mm_right_t(dec_dst[...].astype(BF16), dec_recv[...])
    )
    pre_grad = (hidden_grad * silu_slope(pre_act[...])).astype(BF16)
    put_term(2, mm(grid_in[...], pre_grad))
    scatter_start(1)
    scatter_start(2)
    swap_start(0)
    gather_take(1, lat2_all, 2, n - 1)
    gather_take(3, dsg_all, 1, n)
    gather_take(4, msg_all, 1, n)
    tall = (n * mesh_rows, width)
    decode_grad[...] = mm_left_t(lat2_all[...].reshape(tall), dsg_all[...].reshape(tall))
    process_grad[...] = mm_left_t(lat_all[...].reshape(tall), msg_all[...].reshape(tall))
    swap_end(0, output_grad)
    scatter_end(1)
    scatter_end(2)
    swap_start(1)
    swap_start(2)
    for copy in first + agg_sends + dec_sends + cot_sends:
        copy.wait_send()
    gather_sent(0, lat_all)
    gather_sent(1, lat2_all)
    gather_sent(3, dsg_all)
    gather_sent(4, msg_all)

    @pl.loop(1, n)
    def _(step):
        back_copy(lax.rem(me + step, n), me).wait_send()

    swap_end(1, encode_grad)
    swap_end(2, embed_grad)


def shards(
    grid_in,
    mesh_init,
    embed_weight,
    enc_send,
    enc_recv,
    enc_node,
    mid_send,
    mid_recv,
    mid_node,
    dec_send,
    dec_recv,
    dec_node,
    mid_gain,
    cotangent,
    enc_from,
    enc_into,
    enc_count,
    mid_from,
    mid_into,
    mid_count,
    dec_from,
    dec_into,
    dec_count,
):
    n = lax.axis_size("mesh")
    channels, grid_rows = grid_in.shape
    mesh_rows, width = mesh_init.shape
    span, enc_slots = enc_from.shape
    dec_slots = dec_from.shape[1]
    mid_slots = n * mid_from.shape[1]

    def masked(into, count):
        live = lax.broadcasted_iota(jnp.int32, into.shape, 1) < count[:, None]
        return jnp.where(live, into, -1)

    enc_pack = jnp.concatenate(
        [enc_from, masked(enc_into, enc_count), jnp.zeros((2, enc_slots), jnp.int32)]
    )
    blocks = lax.broadcasted_iota(jnp.int32, mid_from.shape, 0) * mesh_rows
    mid_pack = jnp.stack(
        [(mid_from + blocks).reshape(-1), masked(mid_into, mid_count).reshape(-1)]
    )
    dec_pack = jnp.stack([dec_from, masked(dec_into, dec_count)], axis=1)
    longest = max(width, channels)
    shard = -(-max(16, -(-longest // n)) // 16) * 16
    half = n // 2

    vmem = pltpu.VMEM
    tall = vmem((n, mesh_rows, width), BF16)
    scratch = [
        vmem((grid_rows, width), F32),
        vmem((grid_rows, width), BF16),
        vmem((grid_rows, width), BF16),
        vmem((grid_rows, width), BF16),
        vmem((2,) + enc_pack.shape, jnp.int32),
        vmem((3, mesh_rows, width), BF16),
        vmem((3, enc_slots, width), F32),
        vmem((3, mesh_rows, width), F32),
        vmem((2, mesh_rows, width), F32),
        tall,
        vmem((mid_slots, width), F32),
        tall,
        vmem((3, mesh_rows, width), BF16),
        vmem((3, dec_slots, width), F32),
        vmem((grid_rows, width), BF16),
        vmem((3, mesh_rows, width), F32),
        vmem((2, mesh_rows, width), F32),
        vmem((grid_rows, width), F32),
        tall,
        tall,
        tall,
        tall,
        vmem((3, mesh_rows, width), BF16),
        vmem((grid_rows, width), F32),
        vmem((3, 2, half, shard, width), BF16),
        vmem((3, half, shard, width), BF16),
        vmem((3, half, shard, width), BF16),
        vmem((3, half, shard, width), BF16),
        vmem((3, 2, half, shard, width), BF16),
        vmem((mesh_rows, width), F32),
        vmem((mesh_rows, width), BF16),
        pltpu.SemaphoreType.DMA((5, 2)),
        pltpu.SemaphoreType.DMA((5, 2)),
        pltpu.SemaphoreType.DMA((5, n)),
        pltpu.SemaphoreType.DMA((5, n)),
        pltpu.SemaphoreType.DMA((3, 4)),
        pltpu.SemaphoreType.DMA((3, 2, half)),
        pltpu.SemaphoreType.DMA((3, 2, half)),
    ]
    grad = jax.ShapeDtypeStruct((width, width), F32)
    spec = pl.BlockSpec(memory_space=pltpu.VMEM)
    return pl.pallas_call(
        functools.partial(kernel, n, shard),
        out_shape=(
            jax.ShapeDtypeStruct((grid_rows, width), BF16),
            jax.ShapeDtypeStruct((channels, width), F32),
            grad,
            grad,
            grad,
            grad,
        ),
        in_specs=[spec] * 17,
        out_specs=(spec,) * 6,
        scratch_shapes=scratch,
        compiler_params=pltpu.CompilerParams(
            collective_id=0, has_side_effects=True, vmem_limit_bytes=67043328
        ),
    )(
        grid_in,
        mesh_init,
        embed_weight,
        enc_send,
        enc_recv,
        enc_node,
        mid_send,
        mid_recv,
        mid_node,
        dec_send,
        dec_recv,
        dec_node,
        mid_gain.reshape(1, width),
        cotangent,
        enc_pack,
        mid_pack,
        dec_pack,
    )


def solution(mesh):
    rows = P(("parts", "mesh"), None)
    split = (P("mesh", None), P("mesh", None), P("mesh"))
    return jax.shard_map(
        shards,
        mesh=mesh,
        in_specs=(P(None, ("parts", "mesh")), rows) + (P(),) * 11 + (rows,) + split * 3,
        out_specs=(rows,) + (P("parts", None),) * 5,
        check_vma=False,
    )
```

```python
import functools

import jax
import jax.numpy as jnp
from jax import lax
from jax.experimental import pallas as pl
from jax.experimental.pallas import tpu as pltpu
from jax.sharding import PartitionSpec as P

EPSILON = 1e-05
F32 = jnp.float32
BF16 = jnp.bfloat16


def dot(left, right, dims):
    return lax.dot_general(left, right, (dims, ((), ())), preferred_element_type=F32)


def mm(left, right):
    return dot(left, right, ((1,), (0,)))


def mm_right_t(left, right):
    return dot(left, right, ((1,), (1,)))


def mm_left_t(left, right):
    return dot(left, right, ((0,), (0,)))


def normed(values):
    center = values - jnp.mean(values, axis=-1, keepdims=True)
    scale = lax.rsqrt(jnp.mean(center * center, axis=-1, keepdims=True) + EPSILON)
    return center * scale, scale


def norm_pull(unit, scale, grad):
    inner = jnp.mean(grad * unit, axis=-1, keepdims=True)
    return scale * (grad - jnp.mean(grad, axis=-1, keepdims=True) - unit * inner)


def sigmoid(values):
    return 1.0 / (1.0 + jnp.exp(-values))


def silu(values):
    return values * sigmoid(values)


def silu_slope(values):
    sigma = sigmoid(values)
    return sigma * (1.0 + values * (1.0 - sigma))


def picks(index, rows):
    places = lax.broadcasted_iota(jnp.int32, (rows, index.shape[1]), 0)
    return jnp.where(places == index, 1.0, 0.0).astype(BF16)


def kernel(
    n,
    shard,
    grid_in,
    mesh_init,
    embed_weight,
    enc_send,
    enc_recv,
    enc_node,
    mid_send,
    mid_recv,
    mid_node,
    dec_send,
    dec_recv,
    dec_node,
    mid_gain,
    cotangent,
    enc_from,
    enc_into,
    enc_count,
    mid_pack,
    dec_from,
    dec_into,
    dec_count,
    update,
    embed_grad,
    encode_grad,
    process_grad,
    decode_grad,
    output_grad,
    pre_act,
    hidden,
    enc_proj,
    dec_target,
    packs,
    enc_pack,
    targets,
    enc_inputs,
    agg_parts,
    agg_near,
    lat_all,
    mid_inputs,
    lat2_all,
    dec_near,
    dec_inputs,
    dec_cot,
    dec_parts,
    dec_back,
    dec_dst,
    dsg_all,
    mid_parts,
    mid_back,
    msg_all,
    cots,
    enc_src,
    terms,
    halves,
    paired,
    arrived,
    whole,
    held_grad,
    held_dst,
    near_send,
    near_recv,
    all_send,
    all_recv,
    pair_sem,
    ring_send,
    ring_recv,
):
    me = lax.axis_index("mesh")
    left = lax.rem(me + n - 1, n)
    right = lax.rem(me + 1, n)
    core = lax.rem(me, 2)
    chip = me // 2
    chips = n // 2
    partner = me + 1 - 2 * core
    grid_rows = hidden.shape[0]
    mesh_rows, width = mesh_init.shape

    def remote(src, dst, send, recv, device):
        return pltpu.make_async_remote_copy(
            src_ref=src,
            dst_ref=dst,
            send_sem=send,
            recv_sem=recv,
            device_id={"mesh": device},
            device_id_type=pl.DeviceIdType.MESH,
        )

    def to_left(which, src, dst):
        return remote(src, dst, near_send.at[which, 0], near_recv.at[which, 1], left)

    def to_right(which, src, dst):
        return remote(src, dst, near_send.at[which, 1], near_recv.at[which, 0], right)

    def near_arrive(which, first, second):
        remote(first, first, near_send.at[which, 1], near_recv.at[which, 0], right).wait_recv()
        remote(second, second, near_send.at[which, 0], near_recv.at[which, 1], left).wait_recv()

    def gather_copy(which, table, owner, peer):
        return remote(
            table.at[owner], table.at[owner], all_send.at[which, peer], all_recv.at[which, owner], peer
        )

    def gather_start(which, table):
        @pl.loop(1, n)
        def _(step):
            gather_copy(which, table, me, lax.rem(me + step, n)).start()

    def gather_take(which, table, first, last):
        @pl.loop(first, last)
        def _(step):
            owner = lax.rem(me + step, n)
            gather_copy(which, table, owner, owner).wait_recv()

    def gather_sent(which, table):
        @pl.loop(1, n)
        def _(step):
            gather_copy(which, table, me, lax.rem(me + step, n)).wait_send()

    def pair_copy(k):
        return remote(terms.at[k, 1 - core], halves.at[k], pair_sem.at[k, 0], pair_sem.at[k, 1], partner)

    def ring_copy(k, src, dst, stage, peer, slot):
        return remote(src, dst, ring_send.at[k, stage, peer], ring_recv.at[k, stage, slot], 2 * peer + core)

    def put_term(k, value):
        rows = value.shape[0]
        value = value.astype(BF16)
        for o in range(n):
            low, high = o * shard, min((o + 1) * shard, rows)
            if high - low < shard:
                terms[k, o % 2, o // 2] = jnp.zeros((shard, width), BF16)
            if low < high:
                terms[k, o % 2, o // 2, 0 : high - low] = value[low:high]
        pair_copy(k).start()

    def scatter_start(k):
        pair_copy(k).wait()

        @pl.loop(0, chips)
        def _(i):
            both = terms[k, core, i].astype(F32) + halves[k, i].astype(F32)
            paired[k, i] = both.astype(BF16)

        @pl.loop(1, chips)
        def _(step):
            peer = lax.rem(chip + step, chips)
            ring_copy(k, paired.at[k, peer], arrived.at[k, chip], 0, peer, chip).start()

    def scatter_end(k):
        def add(step, total):
            peer = lax.rem(chip + step, chips)
            ring_copy(k, paired.at[k, peer], arrived.at[k, peer], 0, peer, peer).wait_recv()
            return total + arrived[k, peer].astype(F32)

        total = lax.fori_loop(1, chips, add, paired[k, chip].astype(F32))
        whole[k, core, chip] = total.astype(BF16)

        @pl.loop(1, chips)
        def _(step):
            peer = lax.rem(chip + step, chips)
            mine = whole.at[k, core, chip]
            ring_copy(k, mine, mine, 1, peer, chip).start()

    def final_copy(k, side):
        return remote(whole.at[k, side], whole.at[k, side], pair_sem.at[k, 2], pair_sem.at[k, 3], partner)

    def swap_start(k):
        @pl.loop(1, chips)
        def _(step):
            peer = lax.rem(chip + step, chips)
            theirs = whole.at[k, core, peer]
            ring_copy(k, theirs, theirs, 1, peer, peer).wait_recv()

        final_copy(k, core).start()

    def swap_end(k, out):
        final_copy(k, core).wait_send()
        final_copy(k, 1 - core).wait_recv()
        rows = out.shape[0]
        for o in range(n):
            low, high = o * shard, min((o + 1) * shard, rows)
            if low < high:
                out[low:high] = whole[k, o % 2, o // 2, 0 : high - low]

        @pl.loop(1, chips)
        def _(step):
            peer = lax.rem(chip + step, chips)
            ring_copy(k, paired.at[k, peer], arrived.at[k, chip], 0, peer, chip).wait_send()
            mine = whole.at[k, core, chip]
            ring_copy(k, mine, mine, 1, peer, chip).wait_send()

    barrier = pltpu.get_barrier_semaphore()

    @pl.loop(1, n)
    def _(step):
        pl.semaphore_signal(
            barrier,
            inc=1,
            device_id={"mesh": lax.rem(me + step, n)},
            device_id_type=pl.DeviceIdType.MESH,
        )

    def masked(row, count):
        return jnp.where(lax.broadcasted_iota(jnp.int32, row.shape, 1) < count, row, -1)

    enc_pack[...] = jnp.zeros(enc_pack.shape, jnp.int32)
    enc_pack[0:3] = enc_from[...]
    for j in range(3):
        enc_pack[3 + j : 4 + j] = masked(enc_into[j : j + 1], enc_count[j])
    targets[1] = mm(mesh_init[...], enc_recv[...]).astype(BF16)
    pl.semaphore_wait(barrier, n - 1)
    first = [
        to_left(0, enc_pack, packs.at[1]),
        to_right(0, enc_pack, packs.at[0]),
        to_left(1, targets.at[1], targets.at[2]),
        to_right(1, targets.at[1], targets.at[0]),
    ]
    for copy in first:
        copy.start()

    values = mm_left_t(grid_in[...], embed_weight[...])
    pre_act[...] = values
    hidden[...] = silu(values).astype(BF16)
    enc_proj[...] = mm(hidden[...], enc_send[...]).astype(BF16)
    dec_target[...] = mm(hidden[...], dec_recv[...]).astype(BF16)

    near_arrive(0, packs.at[0], packs.at[1])
    near_arrive(1, targets.at[0], targets.at[2])

    def enc_tables(k):
        pack, row = ((packs[0], 2), (enc_pack[...], 1), (packs[1], 0))[k]
        return (
            picks(pack[row : row + 1], grid_rows),
            picks(pack[row + 3 : row + 4], mesh_rows),
        )

    for k in range(3):
        source, table = enc_tables(k)
        inputs = mm_left_t(source, enc_proj[...]) + mm_left_t(table, targets[k])
        enc_inputs[k] = inputs
        agg_parts[k] = mm(table, silu(inputs).astype(BF16))
    agg_sends = [
        to_left(2, agg_parts.at[0], agg_near.at[1]),
        to_right(2, agg_parts.at[2], agg_near.at[0]),
    ]
    for copy in agg_sends:
        copy.start()
    near_arrive(2, agg_near.at[0], agg_near.at[1])
    enc_unit, enc_scale = normed(agg_parts[1] + agg_near[0] + agg_near[1])
    latent = (mesh_init[...].astype(F32) + mm(enc_unit.astype(BF16), enc_node[...])).astype(BF16)
    lat_all[me] = latent
    gather_start(0, lat_all)
    mid_target = mm(latent, mid_recv[...]).astype(BF16)
    mid_table = picks(mid_pack[1:2], mesh_rows)
    target_at = mm_left_t(mid_table, mid_target)
    gather_take(0, lat_all, 1, n)
    mid_proj = mm(lat_all[...].reshape(n * mesh_rows, width), mid_send[...]).astype(BF16)
    mid_source = picks(mid_pack[0:1], n * mesh_rows)
    inputs = mm_left_t(mid_source, mid_proj) + target_at
    mid_inputs[...] = inputs
    mid_unit, mid_scale = normed(mm(mid_table, silu(inputs).astype(BF16)))
    mid_norm = (mid_unit * mid_gain[...]).astype(BF16)
    latent_two = (latent.astype(F32) + mm(mid_norm, mid_node[...])).astype(BF16)
    lat2_all[me] = latent_two
    gather_start(1, lat2_all)
    dec_near[1] = mm(latent_two, dec_send[...]).astype(BF16)
    gather_take(1, lat2_all, 1, 2)
    gather_take(1, lat2_all, n - 1, n)
    dec_near[0] = mm(lat2_all[left], dec_send[...]).astype(BF16)
    dec_near[2] = mm(lat2_all[right], dec_send[...]).astype(BF16)

    def dec_forward(j, total):
        source = picks(dec_from[pl.ds(j, 1)], mesh_rows)
        table = picks(masked(dec_into[pl.ds(j, 1)], dec_count[j]), grid_rows)
        inputs = mm_left_t(source, dec_near[j]) + mm_left_t(table, dec_target[...])
        dec_inputs[j] = inputs
        return total + mm(table, silu(inputs).astype(BF16))

    dec_agg = lax.fori_loop(0, 3, dec_forward, jnp.zeros((grid_rows, width), F32))
    unit, scale = normed(dec_agg)
    dec_norm = unit.astype(BF16)
    dec_cot[...] = norm_pull(unit, scale, mm_right_t(cotangent[...], dec_node[...])).astype(BF16)
    dec_dst[...] = jnp.zeros((grid_rows, width), F32)

    def dec_backward(j, carry):
        source = picks(dec_from[pl.ds(j, 1)], mesh_rows)
        table = picks(masked(dec_into[pl.ds(j, 1)], dec_count[j]), grid_rows)
        grad = (mm_left_t(table, dec_cot[...]) * silu_slope(dec_inputs[j])).astype(BF16)
        dec_parts[j] = mm(source, grad)
        dec_dst[...] += mm(table, grad)
        return carry

    lax.fori_loop(0, 3, dec_backward, 0)
    dec_sends = [
        to_left(3, dec_parts.at[0], dec_back.at[1]),
        to_right(3, dec_parts.at[2], dec_back.at[0]),
    ]
    for copy in dec_sends:
        copy.start()
    put_term(0, mm_left_t(dec_norm, cotangent[...]))
    update[...] = (hidden[...].astype(F32) + mm(dec_norm, dec_node[...])).astype(BF16)
    near_arrive(3, dec_back.at[0], dec_back.at[1])
    dec_src = (dec_parts[1] + dec_back[0] + dec_back[1]).astype(BF16)
    latent_two_grad = mm_right_t(dec_src, dec_send[...])
    grad = mm_right_t(latent_two_grad.astype(BF16), mid_node[...]) * mid_gain[...]
    mid_cot = norm_pull(mid_unit, mid_scale, grad).astype(BF16)
    grad = (mm_left_t(mid_table, mid_cot) * silu_slope(mid_inputs[...])).astype(BF16)
    mid_parts[...] = mm(mid_source, grad).astype(BF16).reshape(n, mesh_rows, width)

    def back_copy(peer, slot):
        return remote(
            mid_parts.at[peer], mid_back.at[slot], all_send.at[2, peer], all_recv.at[2, slot], peer
        )

    @pl.loop(1, n)
    def _(step):
        back_copy(lax.rem(me + step, n), me).start()

    held_dst[...] = mm(mid_table, grad).astype(BF16)
    held_grad[...] = latent_two_grad
    dsg_all[me] = dec_src
    scatter_start(0)

    def back_add(step, total):
        peer = lax.rem(me + step, n)
        back_copy(peer, peer).wait_recv()
        return total + mid_back[peer].astype(F32)

    mid_src = lax.fori_loop(1, n, back_add, mid_parts[me].astype(F32)).astype(BF16)
    msg_all[me] = mid_src
    latent_grad = (
        held_grad[...]
        + mm_right_t(msg_all[me], mid_send[...])
        + mm_right_t(held_dst[...], mid_recv[...])
    ).astype(BF16)
    enc_cot = norm_pull(enc_unit, enc_scale, mm_right_t(latent_grad, enc_node[...])).astype(BF16)
    cots[1] = enc_cot
    cot_sends = [
        to_left(4, cots.at[1], cots.at[2]),
        to_right(4, cots.at[1], cots.at[0]),
    ]
    for copy in cot_sends:
        copy.start()
    gather_start(3, dsg_all)
    gather_start(4, msg_all)
    scatter_end(0)
    near_arrive(4, cots.at[0], cots.at[2])
    enc_src[...] = jnp.zeros((grid_rows, width), F32)
    for k in range(3):
        source, table = enc_tables(k)
        grad = (mm_left_t(table, cots[k]) * silu_slope(enc_inputs[k])).astype(BF16)
        enc_src[...] += mm(source, grad)
    enc_src_grad = enc_src[...].astype(BF16)
    put_term(1, mm_left_t(hidden[...], enc_src_grad))
    hidden_grad = (
        cotangent[...].astype(F32)
        + mm_right_t(enc_src_grad, enc_send[...])
        + mm_right_t(dec_dst[...].astype(BF16), dec_recv[...])
    )
    pre_grad = (hidden_grad * silu_slope(pre_act[...])).astype(BF16)
    put_term(2, mm(grid_in[...], pre_grad))
    scatter_start(1)
    scatter_start(2)
    swap_start(0)
    gather_take(1, lat2_all, 2, n - 1)
    gather_take(3, dsg_all, 1, n)
    gather_take(4, msg_all, 1, n)
    tall = (n * mesh_rows, width)
    decode_grad[...] = mm_left_t(lat2_all[...].reshape(tall), dsg_all[...].reshape(tall)).astype(BF16)
    process_grad[...] = mm_left_t(lat_all[...].reshape(tall), msg_all[...].reshape(tall)).astype(BF16)
    swap_end(0, output_grad)
    scatter_end(1)
    scatter_end(2)
    swap_start(1)
    swap_start(2)
    for copy in first + agg_sends + dec_sends + cot_sends:
        copy.wait_send()
    gather_sent(0, lat_all)
    gather_sent(1, lat2_all)
    gather_sent(3, dsg_all)
    gather_sent(4, msg_all)

    @pl.loop(1, n)
    def _(step):
        back_copy(lax.rem(me + step, n), me).wait_send()

    swap_end(1, encode_grad)
    swap_end(2, embed_grad)


def shards(
    grid_in,
    mesh_init,
    embed_weight,
    enc_send,
    enc_recv,
    enc_node,
    mid_send,
    mid_recv,
    mid_node,
    dec_send,
    dec_recv,
    dec_node,
    mid_gain,
    cotangent,
    enc_from,
    enc_into,
    enc_count,
    mid_from,
    mid_into,
    mid_count,
    dec_from,
    dec_into,
    dec_count,
):
    n = lax.axis_size("mesh")
    channels, grid_rows = grid_in.shape
    mesh_rows, width = mesh_init.shape
    span, enc_slots = enc_from.shape
    dec_slots = dec_from.shape[1]
    mid_slots = n * mid_from.shape[1]

    def masked(into, count):
        live = lax.broadcasted_iota(jnp.int32, into.shape, 1) < count[:, None]
        return jnp.where(live, into, -1)

    blocks = lax.broadcasted_iota(jnp.int32, mid_from.shape, 0) * mesh_rows
    mid_pack = jnp.stack(
        [(mid_from + blocks).reshape(-1), masked(mid_into, mid_count).reshape(-1)]
    )
    longest = max(width, channels)
    shard = -(-max(16, -(-longest // n)) // 16) * 16
    half = n // 2

    vmem = pltpu.VMEM
    tall = vmem((n, mesh_rows, width), BF16)
    scratch = [
        vmem((grid_rows, width), F32),
        vmem((grid_rows, width), BF16),
        vmem((grid_rows, width), BF16),
        vmem((grid_rows, width), BF16),
        vmem((2, 8, enc_slots), jnp.int32),
        vmem((8, enc_slots), jnp.int32),
        vmem((3, mesh_rows, width), BF16),
        vmem((3, enc_slots, width), F32),
        vmem((3, mesh_rows, width), F32),
        vmem((2, mesh_rows, width), F32),
        tall,
        vmem((mid_slots, width), F32),
        tall,
        vmem((3, mesh_rows, width), BF16),
        vmem((3, dec_slots, width), F32),
        vmem((grid_rows, width), BF16),
        vmem((3, mesh_rows, width), F32),
        vmem((2, mesh_rows, width), F32),
        vmem((grid_rows, width), F32),
        tall,
        tall,
        tall,
        tall,
        vmem((3, mesh_rows, width), BF16),
        vmem((grid_rows, width), F32),
        vmem((3, 2, half, shard, width), BF16),
        vmem((3, half, shard, width), BF16),
        vmem((3, half, shard, width), BF16),
        vmem((3, half, shard, width), BF16),
        vmem((3, 2, half, shard, width), BF16),
        vmem((mesh_rows, width), F32),
        vmem((mesh_rows, width), BF16),
        pltpu.SemaphoreType.DMA((5, 2)),
        pltpu.SemaphoreType.DMA((5, 2)),
        pltpu.SemaphoreType.DMA((5, n)),
        pltpu.SemaphoreType.DMA((5, n)),
        pltpu.SemaphoreType.DMA((3, 4)),
        pltpu.SemaphoreType.DMA((3, 2, half)),
        pltpu.SemaphoreType.DMA((3, 2, half)),
    ]
    grad = jax.ShapeDtypeStruct((width, width), BF16)
    spec = pl.BlockSpec(memory_space=pltpu.VMEM)
    number = pl.BlockSpec(memory_space=pltpu.SMEM)
    update, *grads = pl.pallas_call(
        functools.partial(kernel, n, shard),
        out_shape=(
            jax.ShapeDtypeStruct((grid_rows, width), BF16),
            jax.ShapeDtypeStruct((channels, width), BF16),
            grad,
            grad,
            grad,
            grad,
        ),
        in_specs=[spec] * 16 + [number] + [spec] * 3 + [number],
        out_specs=(spec,) * 6,
        scratch_shapes=scratch,
        compiler_params=pltpu.CompilerParams(
            collective_id=0, has_side_effects=True, vmem_limit_bytes=67043328
        ),
    )(
        grid_in,
        mesh_init,
        embed_weight,
        enc_send,
        enc_recv,
        enc_node,
        mid_send,
        mid_recv,
        mid_node,
        dec_send,
        dec_recv,
        dec_node,
        mid_gain.reshape(1, width),
        cotangent,
        enc_from,
        enc_into,
        enc_count,
        mid_pack,
        dec_from,
        dec_into,
        dec_count,
    )
    return (update,) + tuple(grad.astype(F32) for grad in grads)


def solution(mesh):
    rows = P(("parts", "mesh"), None)
    split = (P("mesh", None), P("mesh", None), P("mesh"))
    return jax.shard_map(
        shards,
        mesh=mesh,
        in_specs=(P(None, ("parts", "mesh")), rows) + (P(),) * 11 + (rows,) + split * 3,
        out_specs=(rows,) + (P("parts", None),) * 5,
        check_vma=False,
    )
```
